32 devices in a mesh: stream: 8 (over z, y), span: 4 (over x, core).
Axes of the slice: x: 2, y: 2, z: 4, core: 2. Of those that a mesh axis runs over, the one named last changes fastest.
Arguments:
- primal_populations: float32 [26, 64, 64, 128], P(None, 'stream', 'span'), may hold values from 0.01 to 0.8, as said below
- adjoint: float32 [26, 64, 64, 128], P(None, 'stream', 'span'), may hold values from -6 to 6
- solid: int32 [64, 64, 128], P('stream', 'span'), may hold values from 0 to 1, as said below
- links: int32 [3, 8, 9856], P(None, 'stream', 'span'), may hold values from 0 to 16384, as said below
Outputs:
- adjoint_next: float32 [26, 64, 64, 128], P(None, 'stream', 'span')
- sensitivity: float32 [128], replicated
The draws below stay inside these ranges and needn't reach their ends.
Inputs may be any that keep to these rules, and one draw needn't show every extreme that they name: `primal_populations`: every entry is positive; in each cell the members 0..18 sum to between 0.5 and 1.5. Every fluid cell beside a solid cell lies on that solid cell's device. `links`: row 0 holds a fluid cell of the device's block, flattened as (x * 16 + y) * 128 + z over its 8 x 16 x 128 cells; row 1 a direction i of 1..18 for which that cell plus c_i is solid; row 2 the owning control point, which on the devices of span index p lies in p * 4 * 2 * 4 .. (p + 1) * 4 * 2 * 4 - 1. Every pair of a fluid cell and a direction toward a solid cell is listed once, on that cell's device. Unused slots hold cell 8 * 16 * 128, direction 0 and control point 128. On some device all 2464 slots are used, on another none.
All inputs are finite; a program needn't handle non-finite values.
Results may differ from the reference program's by a relative error of at most 0.0003.
Values sent between devices are 32-bit elements; how exact they have to be, the bound alone decides.
No kernel may reach another device: no remote copies, remote signals or barrier semaphores. Data moves between devices by JAX's collectives and lax.ppermute only.
A program may use at most 64 MiB of HBM per device.

```python
import jax
import jax.numpy as jnp
import numpy as np
from jax import lax

CX = 8
CY = 16
NZ = 128
BX = 4
SEGMENT_WIDTH = 6
SEGMENT_HEIGHT = 12
PERIOD_PARTS = 4
SEGMENT_CONTROLS = 4
ITERS = 2
SEGMENT_PLACES = 2
LINK_CAP = 2464
NX = 64
NY = 64
PERIODS = 2
NCP = 128


VELOCITY = ((0, 0, 0), (1, 0, 0), (-1, 0, 0), (0, 1, 0), (0, -1, 0), (0, 0, 1), (0, 0, -1), (1, 1, 0), (-1, -1, 0), (1, -1, 0), (-1, 1, 0), (1, 0, 1), (-1, 0, -1), (1, 0, -1), (-1, 0, 1), (0, 1, 1), (0, -1, -1), (0, 1, -1), (0, -1, 1))


ALL_WEIGHTS = (1.0 / 3.0,) + (1.0 / 18.0,) * 6 + (1.0 / 36.0,) * 12 + (0.25,) + (0.125,) * 6


def segment_table():
    entries = []
    for solid_x in range(BX):
        for solid_y in range(SEGMENT_WIDTH):
            for solid_z in range(SEGMENT_HEIGHT):
                for direction in range(1, 19):
                    velocity = VELOCITY[direction]
                    near_x = solid_x - velocity[0]
                    near_y = solid_y - velocity[1]
                    near_z = solid_z - velocity[2]
                    inside = 0 <= near_x < BX and 0 <= near_y < SEGMENT_WIDTH and (0 <= near_z < SEGMENT_HEIGHT)
                    if not inside and near_z >= 0:
                        entries.append((near_x, near_y, near_z, direction, solid_z))
    return np.array(entries, dtype=np.int32)


def design_tables(key):
    base_key = jax.random.fold_in(key, 11)
    subkeys = jax.random.split(base_key, 5)
    devices_period = PERIOD_PARTS * (NY // CY)
    occupied = jax.random.randint(subkeys[0], (devices_period, SEGMENT_PLACES), 0, 10) < 4
    full_dev = jax.random.randint(subkeys[1], (), 0, devices_period)
    empty_dev = (full_dev + 1 + jax.random.randint(subkeys[2], (), 0, devices_period - 1)) % devices_period
    dev_rows = jnp.arange(devices_period, dtype=jnp.int32)[:, None]
    occupied = jnp.where(dev_rows == full_dev, True, jnp.where(dev_rows == empty_dev, False, occupied))
    starts = jax.random.randint(subkeys[3], (devices_period, SEGMENT_PLACES), 1, CX - BX)
    return (occupied, starts, subkeys[4])


def draw_solid(key, part):
    occupied, starts, spare_key = design_tables(key)
    x_cells = jnp.arange(NX, dtype=jnp.int32)
    y_cells = jnp.arange(NY, dtype=jnp.int32)
    z_cells = jnp.arange(NZ, dtype=jnp.int32)
    slab_ids = x_cells // CX % PERIOD_PARTS
    local_x = x_cells % CX
    span_ids = y_cells // CY
    local_y = y_cells % CY
    place_index = local_y // (SEGMENT_WIDTH + 2)
    within_slot = local_y % (SEGMENT_WIDTH + 2)
    part_number = span_ids[None, :] * PERIOD_PARTS + slab_ids[:, None]
    present_mask = occupied[part_number, place_index[None, :]]
    start_x = starts[part_number, place_index[None, :]]
    inside_x = (local_x[:, None] >= start_x) & (local_x[:, None] < start_x + BX)
    inside_y = (within_slot >= 1) & (within_slot < 1 + SEGMENT_WIDTH)
    columns = present_mask & inside_x & inside_y[None, :]
    return (columns[:, :, None] & (z_cells < SEGMENT_HEIGHT)[None, None, :]).astype(jnp.int32)


def draw_links(key, part):
    occupied, starts, shuffle_key = design_tables(key)
    relative_offset = jnp.asarray(segment_table())
    stream_count = NX // CX
    spanwise_count = NY // CY
    stream_ids = jnp.arange(stream_count, dtype=jnp.int32)[:, None]
    span_ids = jnp.arange(spanwise_count, dtype=jnp.int32)[None, :]
    part_number = span_ids * PERIOD_PARTS + stream_ids % PERIOD_PARTS
    place_index = jnp.arange(SEGMENT_PLACES, dtype=jnp.int32)
    present_mask = occupied[part_number][..., None]
    start_x = starts[part_number][..., None]
    near_x = start_x + relative_offset[:, 0]
    near_y = place_index[:, None] * (SEGMENT_WIDTH + 2) + 1 + relative_offset[:, 1]
    cell_ids = (near_x * CY + near_y) * NZ + relative_offset[:, 2]
    direction = jnp.broadcast_to(relative_offset[:, 3], cell_ids.shape)
    owner_parts = ((part_number[..., None] * SEGMENT_PLACES + place_index) * SEGMENT_CONTROLS)[..., None] + relative_offset[:, 4] * SEGMENT_CONTROLS // SEGMENT_HEIGHT
    cell_ids = jnp.where(present_mask, cell_ids, CX * CY * NZ)
    direction = jnp.where(present_mask, direction, 0)
    owner_parts = jnp.where(present_mask, owner_parts, PERIOD_PARTS * spanwise_count * SEGMENT_PLACES * SEGMENT_CONTROLS)
    fields = jnp.stack([cell_ids, direction, owner_parts]).reshape(3, stream_count, spanwise_count, LINK_CAP)
    subkeys = jax.random.split(shuffle_key, stream_count * spanwise_count)
    orders = jax.vmap(lambda one_key: jax.random.permutation(one_key, LINK_CAP))(subkeys)
    orders = orders.reshape(1, stream_count, spanwise_count, LINK_CAP)
    fields = jnp.take_along_axis(fields, jnp.broadcast_to(orders, fields.shape), axis=3)
    return fields.reshape(3, stream_count, spanwise_count * LINK_CAP).astype(jnp.int32)


def draw_primal_populations(key, part):
    first_key, second_key = jax.random.split(key)
    weights = jnp.array(ALL_WEIGHTS, jnp.float32).reshape(26, 1, 1, 1)
    heat_rows = (jnp.arange(26) >= 19).reshape(26, 1, 1, 1)
    spread = jax.random.uniform(first_key, (26, NX, NY, NZ), jnp.float32, 0.7, 1.3)
    heat_level = jax.random.uniform(second_key, (1, NX, NY, NZ), jnp.float32, 0.8, 1.2)
    return weights * spread * jnp.where(heat_rows, heat_level, 1.0)


def steps_of(key, shape, cuts, low, top_value):
    factor_of, own = 1.0, jax.random.fold_in(key, 6)
    for position, blocks in cuts:
        heights = jnp.exp(jax.random.uniform(jax.random.fold_in(own, position), (blocks,), jnp.float32, low / len(cuts), top_value / len(cuts)))
        factor_of = factor_of * jnp.repeat(heights, shape[position] // blocks).reshape([-1 if axis == position else 1 for axis in range(len(shape))])
    return factor_of


def scatter_about(key, extent, scale, bound, pieces=(), held_as=jnp.bfloat16):
    values = jax.random.normal(key, extent, jnp.float32) * scale
    if len(pieces) > 0:
        values = steps_of(key, extent, pieces, -0.22, 0.18) * values
    return jnp.clip(values, min=-bound, max=bound).astype(held_as)


def setup_inputs(seed: int = 0) -> dict:
    key_of = jax.random.split(jax.random.key(seed), 5)
    return {
        "primal_populations": draw_primal_populations(jax.random.fold_in(key_of[4], 71), 0),
        "adjoint": scatter_about(key_of[1], (26, NX, NY, NZ), 1.0, 6.0, ((1, 8), (2, 4)), jnp.float32),
        "solid": draw_solid(jax.random.fold_in(key_of[4], 71), 0),
        "links": draw_links(jax.random.fold_in(key_of[4], 71), 0),
    }


VELOCITY = ((0, 0, 0), (1, 0, 0), (-1, 0, 0), (0, 1, 0), (0, -1, 0), (0, 0, 1), (0, 0, -1),
            (1, 1, 0), (-1, -1, 0), (1, -1, 0), (-1, 1, 0), (1, 0, 1), (-1, 0, -1), (1, 0, -1), (-1, 0, 1),
            (0, 1, 1), (0, -1, -1), (0, 1, -1), (0, -1, 1))
WEIGHTS = (1.0 / 3.0,) + (1.0 / 18.0,) * 6 + (1.0 / 36.0,) * 12
QUADRATURE_HEAT = (0.25,) + (0.125,) * 6
OMEGA_FLOW = 1.0 / 0.6
OMEGA_CONDUCT = 1.25
SENS_SCALE = 0.125


def member_velocity(discrete_direction):
    if discrete_direction < 19:
        return VELOCITY[discrete_direction]
    return VELOCITY[discrete_direction - 19]


def member_opposite(discrete_direction):
    if discrete_direction >= 19:
        return 19 + member_opposite(discrete_direction - 19)
    if discrete_direction == 0:
        return 0
    if discrete_direction % 2 == 1:
        return discrete_direction + 1
    return discrete_direction - 1


def opposite_of(directions):
    return jnp.where(directions == 0, 0, jnp.where(directions % 2 == 1, directions + 1, directions - 1)).astype(jnp.int32)


def dot_velocity(velocity, speed_streamwise_first, speed_transverse_second, speed_vertical_third):
    total = jnp.zeros_like(speed_streamwise_first)
    for coefficient, component_speed in zip(velocity, (speed_streamwise_first, speed_transverse_second, speed_vertical_third)):
        if coefficient != 0:
            total = total + float(coefficient) * component_speed
    return total


def hydrodynamic_sums(population_array):
    mass_per_volume = jnp.sum(population_array[:19], axis=0)
    energy_currents = [jnp.zeros_like(mass_per_volume) for dimension in range(3)]
    for discrete_direction in range(1, 19):
        for dimension in range(3):
            if VELOCITY[discrete_direction][dimension] != 0:
                energy_currents[dimension] = energy_currents[dimension] + float(VELOCITY[discrete_direction][dimension]) * population_array[discrete_direction]
    warmth_grid = jnp.sum(population_array[19:], axis=0)
    return mass_per_volume, energy_currents[0] / mass_per_volume, energy_currents[1] / mass_per_volume, energy_currents[2] / mass_per_volume, warmth_grid


def perform_impact_step(gathered_neighbour_entries, mass_per_volume, speed_streamwise_first, speed_transverse_second, speed_vertical_third, warmth_grid):
    speeds = (speed_streamwise_first, speed_transverse_second, speed_vertical_third)
    square = speed_streamwise_first * speed_streamwise_first + speed_transverse_second * speed_transverse_second + speed_vertical_third * speed_vertical_third
    scalar_sum = jnp.zeros_like(mass_per_volume)
    moment_sum = [jnp.zeros_like(mass_per_volume) for dimension in range(3)]
    for discrete_direction in range(19):
        velocity = VELOCITY[discrete_direction]
        mapped_quantity = dot_velocity(velocity, speed_streamwise_first, speed_transverse_second, speed_vertical_third)
        weighted = WEIGHTS[discrete_direction] * gathered_neighbour_entries[discrete_direction]
        scalar_sum = scalar_sum + weighted * (1.0 + 3.0 * mapped_quantity + 4.5 * mapped_quantity * mapped_quantity - 1.5 * square)
        for dimension in range(3):
            moment_sum[dimension] = moment_sum[dimension] + weighted * (3.0 * velocity[dimension] + 9.0 * mapped_quantity * velocity[dimension] - 3.0 * speeds[dimension])
    heat_sum = jnp.zeros_like(mass_per_volume)
    heat_vector = [jnp.zeros_like(mass_per_volume) for dimension in range(3)]
    for discrete_direction in range(7):
        velocity = VELOCITY[discrete_direction]
        weighted = QUADRATURE_HEAT[discrete_direction] * gathered_neighbour_entries[19 + discrete_direction]
        heat_sum = heat_sum + weighted * (1.0 + 4.0 * dot_velocity(velocity, speed_streamwise_first, speed_transverse_second, speed_vertical_third))
        for dimension in range(3):
            if velocity[dimension] != 0:
                heat_vector[dimension] = heat_vector[dimension] + float(velocity[dimension]) * weighted
    multiplier_coefficient = 4.0 * OMEGA_CONDUCT * warmth_grid / mass_per_volume
    pushed = [OMEGA_FLOW * moment_sum[dimension] + multiplier_coefficient * heat_vector[dimension] for dimension in range(3)]
    offset = OMEGA_FLOW * scalar_sum - (pushed[0] * speed_streamwise_first + pushed[1] * speed_transverse_second + pushed[2] * speed_vertical_third)
    outputs = []
    for discrete_direction in range(19):
        outputs.append((1.0 - OMEGA_FLOW) * gathered_neighbour_entries[discrete_direction] + offset + dot_velocity(VELOCITY[discrete_direction], pushed[0], pushed[1], pushed[2]))
    for discrete_direction in range(7):
        outputs.append((1.0 - OMEGA_CONDUCT) * gathered_neighbour_entries[19 + discrete_direction] + OMEGA_CONDUCT * heat_sum)
    return jnp.stack(outputs)


def postimpact_populations(population_array, mass_per_volume, speed_streamwise_first, speed_transverse_second, speed_vertical_third, warmth_grid):
    square = speed_streamwise_first * speed_streamwise_first + speed_transverse_second * speed_transverse_second + speed_vertical_third * speed_vertical_third
    outputs = []
    for discrete_direction in range(19):
        mapped_quantity = dot_velocity(VELOCITY[discrete_direction], speed_streamwise_first, speed_transverse_second, speed_vertical_third)
        maxwellian_target = WEIGHTS[discrete_direction] * mass_per_volume * (1.0 + 3.0 * mapped_quantity + 4.5 * mapped_quantity * mapped_quantity - 1.5 * square)
        outputs.append(population_array[discrete_direction] - OMEGA_FLOW * (population_array[discrete_direction] - maxwellian_target))
    for discrete_direction in range(7):
        mapped_quantity = dot_velocity(VELOCITY[discrete_direction], speed_streamwise_first, speed_transverse_second, speed_vertical_third)
        maxwellian_target = QUADRATURE_HEAT[discrete_direction] * warmth_grid * (1.0 + 4.0 * mapped_quantity)
        outputs.append(population_array[19 + discrete_direction] - OMEGA_CONDUCT * (population_array[19 + discrete_direction] - maxwellian_target))
    return jnp.stack(outputs)


def shift_zero(section, offset_by, dimension):
    if offset_by == 0:
        return section
    length = section.shape[dimension]
    pad_shape = list(section.shape)
    pad_shape[dimension] = 1
    blank = jnp.zeros(pad_shape, section.dtype)
    if offset_by == 1:
        return jnp.concatenate([lax.slice_in_dim(section, 1, length, axis=dimension), blank], axis=dimension)
    return jnp.concatenate([blank, lax.slice_in_dim(section, 0, length - 1, axis=dimension)], axis=dimension)


def pull_field(field):
    planes = []
    for discrete_direction in range(26):
        velocity = member_velocity(discrete_direction)
        section = jnp.roll(field[discrete_direction], -velocity[0], axis=0)
        section = shift_zero(section, velocity[1], 1)
        section = shift_zero(section, velocity[2], 2)
        planes.append(section)
    return jnp.stack(planes)


def bounce_walls(gathered_neighbour_entries, iterate_snapshot, y_index, y_total, z_index, depth_cells):
    planes = []
    for discrete_direction in range(26):
        velocity = member_velocity(discrete_direction)
        at_wall = None
        if velocity[1] == 1:
            at_wall = y_index == y_total - 1
        elif velocity[1] == -1:
            at_wall = y_index == 0
        if velocity[2] != 0:
            wall_z = (z_index == depth_cells - 1) if velocity[2] == 1 else (z_index == 0)
            at_wall = wall_z if at_wall is None else (at_wall | wall_z)
        if at_wall is None:
            planes.append(gathered_neighbour_entries[discrete_direction])
        else:
            planes.append(jnp.where(at_wall, iterate_snapshot[member_opposite(discrete_direction)], gathered_neighbour_entries[discrete_direction]))
    return jnp.stack(planes)


def reference(primal_populations, adjoint, solid, links):
    cell_count = CX * CY * NZ
    mass_per_volume, speed_streamwise_first, speed_transverse_second, speed_vertical_third, warmth_grid = hydrodynamic_sums(primal_populations)
    liquid_occupied_sites = (1 - solid).astype(jnp.float32)
    cell_ids = links[0]
    directions = links[1]
    owner_parts = links[2]
    usable = cell_ids < cell_count
    safe_cells = jnp.where(usable, cell_ids, 0)
    stream_ids = lax.broadcasted_iota(jnp.int32, cell_ids.shape, 0)
    span_ids = lax.broadcasted_iota(jnp.int32, cell_ids.shape, 1) // LINK_CAP
    global_x = (stream_ids * CX + safe_cells // (CY * NZ)).astype(jnp.int32)
    global_y = (span_ids * CY + (safe_cells // NZ) % CY).astype(jnp.int32)
    global_z = (safe_cells % NZ).astype(jnp.int32)
    opposite = opposite_of(directions)
    axis_link = usable & (directions >= 1) & (directions <= 6)
    flow_slot = jnp.where(usable, directions, 26).astype(jnp.int32)
    heat_slot = jnp.where(axis_link, 19 + directions, 26).astype(jnp.int32)
    heat_source = jnp.where(axis_link, 19 + opposite, 0).astype(jnp.int32)
    y_index = lax.broadcasted_iota(jnp.int32, (1, NY, 1), 1)
    z_index = lax.broadcasted_iota(jnp.int32, (1, 1, NZ), 2)
    iterate_snapshot = adjoint
    sensitivity = jnp.zeros((NCP,), jnp.float32)
    for iteration in range(ITERS):
        flow_back = iterate_snapshot[opposite, global_x, global_y, global_z]
        heat_back = 1.0 - iterate_snapshot[heat_source, global_x, global_y, global_z]
        if iteration == ITERS - 1:
            gathered = primal_populations[:, global_x, global_y, global_z]
            link_density, link_x, link_y, link_z, link_heat = hydrodynamic_sums(gathered)
            post_state = postimpact_populations(gathered, link_density, link_x, link_y, link_z, link_heat)
            row_ids = lax.broadcasted_iota(jnp.int32, post_state.shape, 0)
            flow_pick = jnp.sum(jnp.where(row_ids == directions[None], post_state, 0.0), axis=0)
            heat_pick = jnp.sum(jnp.where(row_ids == 19 + directions[None], post_state, 0.0), axis=0)
            link_terms = jnp.where(usable, flow_pick * flow_back, 0.0) + jnp.where(axis_link, heat_pick * heat_back, 0.0)
            target = jnp.where(usable, owner_parts, NCP).astype(jnp.int32)
            sensitivity = jnp.zeros((NCP,), jnp.float32).at[target.reshape(-1)].add(link_terms.reshape(-1), mode="drop")
            sensitivity = sensitivity * (SENS_SCALE / PERIODS)
        gathered_neighbour_entries = pull_field(iterate_snapshot)
        gathered_neighbour_entries = bounce_walls(gathered_neighbour_entries, iterate_snapshot, y_index, NY, z_index, NZ)
        gathered_neighbour_entries = gathered_neighbour_entries.at[flow_slot, global_x, global_y, global_z].set(flow_back, mode="drop")
        gathered_neighbour_entries = gathered_neighbour_entries.at[heat_slot, global_x, global_y, global_z].set(heat_back, mode="drop")
        iterate_snapshot = perform_impact_step(gathered_neighbour_entries, mass_per_volume, speed_streamwise_first, speed_transverse_second, speed_vertical_third, warmth_grid) * liquid_occupied_sites[None]
    return iterate_snapshot, sensitivity
```

```python
import functools

import jax
import jax.numpy as jnp
from jax import lax
from jax.experimental import pallas as pl
from jax.experimental.pallas import tpu as pltpu
from jax.sharding import PartitionSpec as P

SEGMENT_WIDTH = 6
PERIOD_PARTS = 4
SEGMENT_CONTROLS = 4
SENS_SCALE = 0.125

VELOCITY = (
    (0, 0, 0),
    (1, 0, 0),
    (-1, 0, 0),
    (0, 1, 0),
    (0, -1, 0),
    (0, 0, 1),
    (0, 0, -1),
    (1, 1, 0),
    (-1, -1, 0),
    (1, -1, 0),
    (-1, 1, 0),
    (1, 0, 1),
    (-1, 0, -1),
    (1, 0, -1),
    (-1, 0, 1),
    (0, 1, 1),
    (0, -1, -1),
    (0, 1, -1),
    (0, -1, 1),
)
C = VELOCITY + VELOCITY[:7]
WEIGHTS = (1.0 / 3.0,) + (1.0 / 18.0,) * 6 + (1.0 / 36.0,) * 12
HEAT = (0.25,) + (0.125,) * 6
OMEGA_F = 1.0 / 0.6
OMEGA_T = 1.25
MEMBERS = 26


def opp(m):
    if m >= 19:
        return 19 + opp(m - 19)
    return 0 if m == 0 else m + 1 if m % 2 else m - 1


def movers(axis, sign):
    return [m for m in range(MEMBERS) if C[m][axis] == sign]


XP, XM, YP, YM = movers(0, 1), movers(0, -1), movers(1, 1), movers(1, -1)
FACE = len(XP)

GROUP, BITS = 4, 6
GROUPS = -(-18 // GROUP)


def place(i):
    return (i - 1) // GROUP, BITS * ((i - 1) % GROUP)


def plus(*terms):
    terms = [t for t in terms if t is not None]
    return functools.reduce(lambda a, b: a + b, terms) if terms else None


def minus(a, b):
    if b is None:
        return a
    return -b if a is None else a - b


def times(c, a):
    return None if a is None or c is None else c * a


def collide(b, u, coef, fluid, wanted):
    g = b.get
    a = {i: plus(g(i), g(i + 1)) for i in range(1, 19, 2)}
    d = {i: minus(g(i), g(i + 1)) for i in range(1, 19, 2)}
    w0, w1, w2 = WEIGHTS[0], WEIGHTS[1], WEIGHTS[7]
    xy, xz, yz = plus(a[7], a[9]), plus(a[11], a[13]), plus(a[15], a[17])
    s0 = plus(times(w0, g(0)), times(w1, plus(a[1], a[3], a[5])), times(w2, plus(xy, xz, yz)))
    s1 = [
        plus(times(w1, d[1]), times(w2, plus(d[7], d[9], d[11], d[13]))),
        plus(times(w1, d[3]), times(w2, plus(minus(d[7], d[9]), d[15], d[17]))),
        plus(times(w1, d[5]), times(w2, plus(minus(d[11], d[13]), minus(d[15], d[17])))),
    ]
    sxx = plus(times(w1, a[1]), times(w2, plus(xy, xz)))
    syy = plus(times(w1, a[3]), times(w2, plus(xy, yz)))
    szz = plus(times(w1, a[5]), times(w2, plus(xz, yz)))
    sxy = times(w2, minus(a[7], a[9]))
    sxz = times(w2, minus(a[11], a[13]))
    syz = times(w2, minus(a[15], a[17]))
    rows = ((sxx, sxy, sxz), (sxy, syy, syz), (sxz, syz, szz))
    s2u = [plus(*(times(e, v) for e, v in zip(row, u))) for row in rows]
    dot = lambda p, q: plus(*(times(e, v) for e, v in zip(p, q)))
    uu = u[0] * u[0] + u[1] * u[1] + u[2] * u[2]
    m0 = plus(times(1.0 - 1.5 * uu, s0), times(3.0, dot(s1, u)), times(4.5, dot(s2u, u)))
    m = [
        minus(plus(times(3.0, s1[k]), times(9.0, s2u[k])), times(3.0, times(u[k], s0)))
        for k in range(3)
    ]
    t0 = plus(
        times(HEAT[0], g(19)), times(HEAT[1], plus(*(g(20 + k) for k in range(6))))
    )
    t1 = [times(HEAT[1], minus(g(20 + 2 * k), g(21 + 2 * k))) for k in range(3)]
    s = plus(t0, times(4.0, dot(t1, u)))
    p = [plus(times(OMEGA_F, m[k]), times(coef, t1[k])) for k in range(3)]
    base = times(fluid, minus(times(OMEGA_F, m0), dot(p, u)))
    p = [times(fluid, e) for e in p]
    relax_f, relax_t = (1.0 - OMEGA_F) * fluid, (1.0 - OMEGA_T) * fluid
    heat = times(fluid, times(OMEGA_T, s))
    out = {}
    for i in wanted:
        if i < 19:
            value = plus(times(relax_f, g(i)), base)
            for k in range(3):
                if C[i][k] == 1:
                    value = plus(value, p[k])
                elif C[i][k] == -1:
                    value = minus(value, p[k])
            out[i] = value
        else:
            out[i] = plus(times(relax_t, g(i)), heat)
    return out


def wall_of(m, rows, lanes, y_first, y_last):
    mask = None
    if C[m][1] != 0:
        mask = rows == (y_last if C[m][1] == 1 else y_first)
    if C[m][2] != 0:
        edge = lanes == (lanes.shape[1] - 1 if C[m][2] == 1 else 0)
        mask = edge if mask is None else mask | edge
    return mask


def shifted(slab, m, fill, rows):
    count, width = slab.shape
    if C[m][1] == 1:
        slab = jnp.where(rows == count - 1, fill, pltpu.roll(slab, count - 1, 0))
    elif C[m][1] == -1:
        slab = jnp.where(rows == 0, fill, pltpu.roll(slab, 1, 0))
    if C[m][2] != 0:
        slab = pltpu.roll(slab, width - 1 if C[m][2] == 1 else 1, 1)
    return slab


def bounce(m, own, pulled, link, wall):
    pulled = jnp.zeros_like(own) if pulled is None else pulled
    if m < 19:
        return jnp.where(link if wall is None else link | wall, own, pulled)
    if wall is not None:
        pulled = jnp.where(wall, own, pulled)
    return jnp.where(link, 1.0 - own, pulled)


def link_mask(packed, x, m):
    group, low = place(m if m < 19 else m - 19)
    return (packed[group, x] & (((1 << BITS) - 1) << low)) != 0


def indices(shape):
    return (
        lax.broadcasted_iota(jnp.int32, shape, 0),
        lax.broadcasted_iota(jnp.int32, shape, 1),
    )


def pick(even, first, second):
    return jnp.where(even, first, second)


SPAN_EVEN, STREAM_EVEN, Y_FIRST, Y_LAST, CONTROL = range(5)


def pack_span_kernel(info, field, out_a, out_b, lo, hi, sems):
    rows = field.shape[2]
    copies = []
    for k in range(FACE):
        copies.append(pltpu.make_async_copy(field.at[YP[k], :, 0], lo.at[k], sems.at[k]))
        copies.append(
            pltpu.make_async_copy(field.at[YM[k], :, rows - 1], hi.at[k], sems.at[FACE + k])
        )
    for copy in copies:
        copy.start()
    for copy in copies:
        copy.wait()
    even = info[SPAN_EVEN] == 1
    for k in range(FACE):
        out_a[k] = pick(even, hi[k], lo[k])
        out_b[k] = pick(even, lo[k], hi[k])
    out_a[FACE] = jnp.zeros_like(out_a[FACE])
    out_b[FACE] = jnp.zeros_like(out_b[FACE])


def prepare_kernel(info, primal, solid, links, state, packed, span_of, slots):
    count_x, count_y, depth = solid.shape
    cells = count_x * count_y * depth
    for x in range(count_x):
        f = [primal[m, x] for m in range(MEMBERS)]
        rho = plus(*f[:19])
        inverse = 1.0 / rho
        momentum = [
            minus(plus(*(f[i] for i in range(1, 19) if C[i][k] == 1)),
                  plus(*(f[i] for i in range(1, 19) if C[i][k] == -1)))
            for k in range(3)
        ]
        theta = plus(*f[19:])
        for k in range(3):
            state[k, x] = momentum[k] * inverse
        state[3, x] = (4.0 * OMEGA_T) * theta * inverse
        state[4, x] = (1 - solid[x]).astype(jnp.float32)
        state[5, x] = rho
        state[6, x] = theta
    given = links.shape[2]
    slots[...] = jnp.full(slots.shape, cells, jnp.int32)
    for k in range(3):
        slots[k : k + 1, 0:given] = links[k]
    cell, direction = slots[0:1, :], slots[1:2, :]
    control = slots[2:3, :] - info[CONTROL]
    used = cell < cells
    span_of[0] = jnp.min(jnp.where(used, control, 1 << 20))
    span_of[1] = jnp.max(jnp.where(used, control, -1))
    total = slots.shape[1]
    column = lax.shift_right_logical(cell, depth.bit_length() - 1)
    height = cell & (depth - 1)
    columns = count_x * count_y
    on_column = lax.broadcasted_iota(jnp.int32, (columns, total), 0) == column
    on_height = jnp.where(
        (lax.broadcasted_iota(jnp.int32, (depth, total), 0) == height) & used, 1.0, 0.0
    ).astype(jnp.bfloat16)
    for group in range(GROUPS):
        code = jnp.zeros((1, total), jnp.float32)
        for i in range(1, 19):
            if place(i)[0] == group:
                value = (control + 1).astype(jnp.float32) * float(1 << place(i)[1])
                code = jnp.where(direction == i, value, code)
        left = jnp.where(on_column, code, 0.0).astype(jnp.bfloat16)
        dense = lax.dot_general(
            left, on_height, (((1,), (1,)), ((), ())), preferred_element_type=jnp.float32
        )
        packed[group] = dense.astype(jnp.int32).reshape(count_x, count_y, depth)


def message_rows(count_y):
    return (2 * FACE + 5) * count_y + 8


def gather_pull(field, halo_lo, halo_hi, x, m, rows, beyond_lo=None, beyond_hi=None):
    count_x = halo_lo.shape[1] if hasattr(halo_lo, "shape") else 0
    at = x + C[m][0]
    if at < 0 or at >= count_x:
        beyond = beyond_lo if at < 0 else beyond_hi
        if beyond is None:
            return None
        slab, fill = beyond(m)
    else:
        slab = field(m, at)
        fill = None
        if C[m][1] == 1:
            fill = halo_hi[YP.index(m), at : at + 1]
        elif C[m][1] == -1:
            fill = halo_lo[YM.index(m), at : at + 1]
    return shifted(slab, m, fill, rows)


def advance_slab(field, halo_lo, halo_hi, state, packed, x, info, beyond_lo=None, beyond_hi=None):
    rows, lanes = indices(state.shape[2:])
    b = {0: field(0, x), 19: field(19, x)}
    for m in range(MEMBERS):
        if m in (0, 19):
            continue
        pulled = gather_pull(field, halo_lo, halo_hi, x, m, rows, beyond_lo, beyond_hi)
        wall = wall_of(m, rows, lanes, info[Y_FIRST], info[Y_LAST])
        b[m] = bounce(m, field(opp(m), x), pulled, link_mask(packed, x, m), wall)
    u = [state[k, x] for k in range(3)]
    return collide(b, u, state[3, x], state[4, x], range(MEMBERS))


def select_halos(even, recv_a, recv_b, lo, hi):
    hi[...] = pick(even, recv_a[...], recv_b[...])
    lo[...] = pick(even, recv_b[...], recv_a[...])


def edge_kernel(info, adjoint, recv_a, recv_b, state, packed, edge, out_a, out_b, lo, hi):
    count_x, count_y = state.shape[1:3]
    select_halos(info[SPAN_EVEN] == 1, recv_a, recv_b, lo, hi)
    field = lambda m, x: adjoint[m, x]
    even = info[STREAM_EVEN] == 1
    for side, x, sent, flagged in ((0, 0, XP, XM), (1, count_x - 1, XM, XP)):
        out = advance_slab(field, lo, hi, state, packed, x, info)
        for m in range(MEMBERS):
            edge[side, m] = out[m]
        flags = state[4, x].astype(jnp.int32)
        for k, m in enumerate(flagged[: FACE - 1]):
            flags = flags + jnp.where(link_mask(packed, x, m), 2 << k, 0)
        parts = [adjoint[m, x] for m in sent] + [out[m] for m in sent]
        parts += [state[k, x] for k in range(4)] + [flags.astype(jnp.float32)]
        down = [m for m in sent if C[m][1] == -1][0]
        up = [m for m in sent if C[m][1] == 1][0]
        below, above = lo[YM.index(down), x : x + 1], hi[YP.index(up), x : x + 1]
        tail = jnp.concatenate(
            [below, above, jnp.zeros((6, below.shape[1]), jnp.float32)], axis=0
        )
        first = even if side == 1 else jnp.logical_not(even)

        def write(target):
            for k, part in enumerate(parts):
                target[k * count_y : (k + 1) * count_y] = part
            target[len(parts) * count_y : len(parts) * count_y + 8] = tail

        @pl.when(first)
        def _():
            write(out_a)

        @pl.when(jnp.logical_not(first))
        def _():
            write(out_b)


def interior_kernel(info, adjoint, recv_a, recv_b, state, packed, inner, lo, hi):
    count_x = state.shape[1]
    select_halos(info[SPAN_EVEN] == 1, recv_a, recv_b, lo, hi)
    field = lambda m, x: adjoint[m, x]
    for x in range(1, count_x - 1):
        out = advance_slab(field, lo, hi, state, packed, x, info)
        for m in range(MEMBERS):
            inner[m, x - 1] = out[m]


def correct_kernel(
    info, adjoint, span_a, span_b, recv_a, recv_b, state, packed, edge, inner,
    fixed, ring, out_a, out_b, lo, hi, message, send,
):
    count_x, count_y = state.shape[1:3]
    select_halos(info[SPAN_EVEN] == 1, span_a, span_b, lo, hi)
    even = info[STREAM_EVEN] == 1
    message[1] = pick(even, recv_a[...], recv_b[...])
    message[0] = pick(even, recv_b[...], recv_a[...])
    rows, lanes = indices(state.shape[2:])
    for side, x, came, went in ((0, 0, XM, XP), (1, count_x - 1, XP, XM)):
        part = lambda k: message[side, k * count_y : (k + 1) * count_y]
        tail = (2 * FACE + 5) * count_y
        b = {}
        for k, m in enumerate(came):
            row = tail if C[m][1] == -1 else tail + 1
            fill = message[side, row : row + 1] if C[m][1] != 0 else None
            pulled = shifted(part(k), m, fill, rows)
            blocked = link_mask(packed, x, m)
            wall = wall_of(m, rows, lanes, info[Y_FIRST], info[Y_LAST])
            blocked = blocked if wall is None else blocked | wall
            b[m] = jnp.where(blocked, 0.0, pulled)
        u = [state[k, x] for k in range(3)]
        out = collide(b, u, state[3, x], state[4, x], range(MEMBERS))
        for m in range(MEMBERS):
            fixed[side, m] = edge[side, m] + out[m]
        u = [part(2 * FACE + k) for k in range(3)]
        flags = part(2 * FACE + 4).astype(jnp.int32)
        b = {}
        for k, m in enumerate(went):
            fill = None
            if C[m][1] == 1:
                fill = hi[YP.index(m), x : x + 1]
            elif C[m][1] == -1:
                fill = lo[YM.index(m), x : x + 1]
            pulled = shifted(adjoint[m, x], m, fill, rows)
            blocked = (flags & (2 << (k % (FACE - 1)))) != 0
            wall = wall_of(m, rows, lanes, info[Y_FIRST], info[Y_LAST])
            blocked = blocked if wall is None else blocked | wall
            b[m] = jnp.where(blocked, 0.0, pulled)
        fluid = (flags & 1).astype(jnp.float32)
        out = collide(b, u, part(2 * FACE + 3), fluid, came)
        for k, m in enumerate(came):
            ring[side, k] = part(FACE + k) + out[m]
    last = count_y - 1
    for side, group, row in ((0, YP, 0), (1, YM, last)):
        for k, m in enumerate(group):
            send[side, k, 0:1] = fixed[0, m, row : row + 1]
            send[side, k, count_x - 1 : count_x] = fixed[1, m, row : row + 1]
            for x in range(1, count_x - 1):
                send[side, k, x : x + 1] = inner[m, x - 1, row : row + 1]
        send[side, FACE] = jnp.zeros((count_x, state.shape[3]), jnp.float32)
        for end, came in ((0, XM), (1, XP)):
            m = [e for e in came if e in group][0]
            send[side, FACE, end : end + 1] = ring[end, came.index(m), row : row + 1]
    span_even = info[SPAN_EVEN] == 1
    out_a[...] = pick(span_even, send[1], send[0])
    out_b[...] = pick(span_even, send[0], send[1])


CHUNK = 4


def sensitivity_kernel(info, span_of, primal, state, packed, fixed, inner, out, values, owners, acc):
    count_x, count_y, depth = state.shape[1:]

    def field(m, x):
        if x == 0 or x == count_x - 1:
            return fixed[0 if x == 0 else 1, m]
        return inner[m, x - 1]

    for x in range(count_x):
        u = [state[k, x] for k in range(3)]
        rho, theta = state[5, x], state[6, x]
        base = 1.0 - 1.5 * (u[0] * u[0] + u[1] * u[1] + u[2] * u[2])
        for i in range(1, 19):
            cu = None
            for k in range(3):
                cu = plus(cu, u[k]) if C[i][k] == 1 else minus(cu, u[k]) if C[i][k] == -1 else cu
            target = (OMEGA_F * WEIGHTS[i]) * rho * (base + cu * (3.0 + 4.5 * cu))
            value = ((1.0 - OMEGA_F) * primal[i, x] + target) * field(opp(i), x)
            if i <= 6:
                target = (OMEGA_T * HEAT[i]) * theta * (1.0 + 4.0 * cu)
                heat = (1.0 - OMEGA_T) * primal[19 + i, x] + target
                value = value + heat * (1.0 - field(19 + opp(i), x))
            group, low = place(i)
            owner = lax.shift_right_logical(packed[group, x], low) & ((1 << BITS) - 1)
            at = ((i - 1) * count_x + x) * count_y
            values[at : at + count_y] = value
            owners[at : at + count_y] = owner - 1
    acc[...] = jnp.zeros_like(acc)
    first, last = span_of[0], span_of[1]
    passes = lax.div(jnp.maximum(last - first + CHUNK, 0), CHUNK)
    step = 64

    def one_pass(j, carry):
        q = first + j * CHUNK

        def block(n, sums):
            sums = list(sums)
            start = pl.multiple_of(n * step, step)
            for t in range(step // 8):
                v = values[pl.ds(start + 8 * t, 8)]
                o = owners[pl.ds(start + 8 * t, 8)]
                for c in range(CHUNK):
                    sums[c] = sums[c] + jnp.where(o == q + c, v, 0.0)
            return tuple(sums)

        zero = jnp.zeros((8, depth), jnp.float32)
        sums = lax.fori_loop(0, values.shape[0] // step, block, (zero,) * CHUNK)
        for c in range(CHUNK):
            row = jnp.minimum(info[CONTROL] + q + c, acc.shape[0] - 1)
            inside = (q + c <= last).astype(jnp.float32)
            acc[pl.ds(row, 1)] = acc[pl.ds(row, 1)] + inside * jnp.sum(
                sums[c], axis=0, keepdims=True
            )
        return carry

    lax.fori_loop(0, passes, one_pass, 0)
    out[...] = lax.dot_general(
        jnp.ones((8, depth), jnp.float32),
        acc[...],
        (((1,), (1,)), ((), ())),
        precision=lax.Precision.HIGHEST,
        preferred_element_type=jnp.float32,
    )


def final_kernel(info, fixed, inner, ring, span_a, span_b, state, packed, out, lo, hi):
    count_x = state.shape[1]
    select_halos(info[SPAN_EVEN] == 1, span_a, span_b, lo, hi)

    def field(m, x):
        if x == 0 or x == count_x - 1:
            return fixed[0 if x == 0 else 1, m]
        return inner[m, x - 1]

    def beyond(end, came, m):
        fill = None
        if C[m][1] != 0:
            fill = (hi if C[m][1] == 1 else lo)[FACE, end : end + 1]
        return ring[end, came.index(m)], fill

    for x in range(count_x):
        result = advance_slab(
            field, lo, hi, state, packed, x, info,
            functools.partial(beyond, 0, XM), functools.partial(beyond, 1, XP),
        )
        for m in range(MEMBERS):
            out[m, x] = result[m]


def vmem():
    return pl.BlockSpec(memory_space=pltpu.VMEM)


def smem():
    return pl.BlockSpec(memory_space=pltpu.SMEM)


def f32(*shape):
    return jax.ShapeDtypeStruct(shape, jnp.float32)


def run(kernel, inputs, in_specs, outs, scratch=(), out_specs=None, limit=None):
    nbytes = sum(4 * e.size for e in inputs) + sum(4 * e.size for e in outs)
    return pl.pallas_call(
        kernel,
        out_shape=tuple(outs),
        in_specs=in_specs,
        out_specs=tuple(out_specs or [vmem()] * len(outs)),
        scratch_shapes=list(scratch),
        cost_estimate=pl.CostEstimate(
            flops=2 * nbytes, bytes_accessed=nbytes, transcendentals=0
        ),
        compiler_params=pltpu.CompilerParams(vmem_limit_bytes=limit),
    )(*inputs)


def swap_pairs(count, start, closed):
    pairs = []
    for i in range(start, count if closed else count - 1, 2):
        j = (i + 1) % count
        pairs += [(i, j), (j, i)]
    return pairs


def swap(parts, axis, closed):
    count = lax.axis_size(axis)
    assert count % 2 == 0
    return [
        lax.ppermute(part, axis, swap_pairs(count, start, closed))
        for start, part in enumerate(parts)
    ]


def shards(primal, adjoint, solid, links):
    members, count_x, count_y, depth = adjoint.shape
    assert members == MEMBERS and depth == 128 and count_y % 8 == 0
    stream_count, span_count = lax.axis_size("stream"), lax.axis_size("span")
    span, stream = lax.axis_index("span"), lax.axis_index("stream")
    share = PERIOD_PARTS * (count_y // (SEGMENT_WIDTH + 2)) * SEGMENT_CONTROLS
    controls = share * span_count
    assert share < (1 << BITS) - 1 and controls <= depth
    info = jnp.stack(
        [
            1 - span % 2,
            1 - stream % 2,
            jnp.where(span == 0, 0, -1),
            jnp.where(span == span_count - 1, count_y - 1, -1),
            span * share,
        ]
    ).astype(jnp.int32)
    row = (count_x, depth)
    halo = f32(FACE + 1, *row)
    halo_scratch = [pltpu.VMEM(halo.shape, jnp.float32)] * 2
    slab = (count_y, depth)

    span_a, span_b = swap(
        run(
            pack_span_kernel,
            [info, adjoint],
            [smem(), pl.BlockSpec(memory_space=pl.ANY)],
            [halo, halo],
            [pltpu.VMEM((FACE, *row), jnp.float32)] * 2 + [pltpu.SemaphoreType.DMA((2 * FACE,))],
        ),
        "span",
        False,
    )
    slots = -(-links.shape[2] // 128) * 128
    state, packed, span_of = run(
        prepare_kernel,
        [info, primal, solid, links],
        [smem(), vmem(), vmem(), vmem()],
        [
            f32(7, count_x, *slab),
            jax.ShapeDtypeStruct((GROUPS, count_x, *slab), jnp.int32),
            jax.ShapeDtypeStruct((2,), jnp.int32),
        ],
        [pltpu.VMEM((8, slots), jnp.int32)],
        [vmem(), vmem(), smem()],
    )
    message = f32(message_rows(count_y), depth)
    edge, *parts = run(
        edge_kernel,
        [info, adjoint, span_a, span_b, state, packed],
        [smem()] + [vmem()] * 5,
        [f32(2, MEMBERS, *slab), message, message],
        halo_scratch,
    )
    stream_a, stream_b = swap(parts, "stream", True)
    (inner,) = run(
        interior_kernel,
        [info, adjoint, span_a, span_b, state, packed],
        [smem()] + [vmem()] * 5,
        [f32(MEMBERS, count_x - 2, *slab)],
        halo_scratch,
    )
    fixed, ring, *parts = run(
        correct_kernel,
        [info, adjoint, span_a, span_b, stream_a, stream_b, state, packed, edge, inner],
        [smem()] + [vmem()] * 9,
        [f32(2, MEMBERS, *slab), f32(2, FACE, *slab), halo, halo],
        halo_scratch
        + [
            pltpu.VMEM((2, *message.shape), jnp.float32),
            pltpu.VMEM((2, *halo.shape), jnp.float32),
        ],
    )
    next_a, next_b = swap(parts, "span", False)
    (partial,) = run(
        sensitivity_kernel,
        [info, span_of, primal, state, packed, fixed, inner],
        [smem(), smem()] + [vmem()] * 5,
        [f32(8, depth)],
        [
            pltpu.VMEM((18 * count_x * count_y, depth), jnp.float32),
            pltpu.VMEM((18 * count_x * count_y, depth), jnp.int32),
            pltpu.VMEM((depth, depth), jnp.float32),
        ],
    )
    everyone = stream_count * span_count
    copies = jnp.broadcast_to(partial[:1], (everyone, depth))
    copies = lax.all_to_all(copies, ("stream", "span"), 0, 0, tiled=True)
    sensitivity = jnp.sum(copies, axis=0)[:controls] * (
        SENS_SCALE / (stream_count // PERIOD_PARTS)
    )
    (result,) = run(
        final_kernel,
        [info, fixed, inner, ring, next_a, next_b, state, packed],
        [smem()] + [vmem()] * 7,
        [f32(MEMBERS, count_x, *slab)],
        halo_scratch,
    )
    return result, sensitivity


def solution(mesh):
    placed = (
        P(None, "stream", "span", None),
        P(None, "stream", "span", None),
        P("stream", "span", None),
        P(None, "stream", "span"),
    )
    return jax.shard_map(
        shards,
        mesh=mesh,
        in_specs=placed,
        out_specs=(P(None, "stream", "span", None), P()),
        check_vma=False,
    )
```

```python
import functools

import jax
import jax.numpy as jnp
from jax import lax
from jax.experimental import pallas as pl
from jax.experimental.pallas import tpu as pltpu
from jax.sharding import PartitionSpec as P

SEGMENT_WIDTH = 6
PERIOD_PARTS = 4
SEGMENT_CONTROLS = 4
SENS_SCALE = 0.125

VELOCITY = (
    (0, 0, 0),
    (1, 0, 0),
    (-1, 0, 0),
    (0, 1, 0),
    (0, -1, 0),
    (0, 0, 1),
    (0, 0, -1),
    (1, 1, 0),
    (-1, -1, 0),
    (1, -1, 0),
    (-1, 1, 0),
    (1, 0, 1),
    (-1, 0, -1),
    (1, 0, -1),
    (-1, 0, 1),
    (0, 1, 1),
    (0, -1, -1),
    (0, 1, -1),
    (0, -1, 1),
)
C = VELOCITY + VELOCITY[:7]
WEIGHTS = (1.0 / 3.0,) + (1.0 / 18.0,) * 6 + (1.0 / 36.0,) * 12
HEAT = (0.25,) + (0.125,) * 6
OMEGA_F = 1.0 / 0.6
OMEGA_T = 1.25
MEMBERS = 26


def opp(m):
    if m >= 19:
        return 19 + opp(m - 19)
    return 0 if m == 0 else m + 1 if m % 2 else m - 1


def movers(axis, sign):
    return [m for m in range(MEMBERS) if C[m][axis] == sign]


XP, XM, YP, YM = movers(0, 1), movers(0, -1), movers(1, 1), movers(1, -1)
FACE = len(XP)

GROUP, BITS = 4, 6
GROUPS = -(-18 // GROUP)


def place(i):
    return (i - 1) // GROUP, BITS * ((i - 1) % GROUP)


def plus(*terms):
    terms = [t for t in terms if t is not None]
    return functools.reduce(lambda a, b: a + b, terms) if terms else None


def minus(a, b):
    if b is None:
        return a
    return -b if a is None else a - b


def times(c, a):
    return None if a is None or c is None else c * a


def collide(b, u, coef, fluid, wanted):
    g = b.get
    a = {i: plus(g(i), g(i + 1)) for i in range(1, 19, 2)}
    d = {i: minus(g(i), g(i + 1)) for i in range(1, 19, 2)}
    w0, w1, w2 = WEIGHTS[0], WEIGHTS[1], WEIGHTS[7]
    xy, xz, yz = plus(a[7], a[9]), plus(a[11], a[13]), plus(a[15], a[17])
    s0 = plus(times(w0, g(0)), times(w1, plus(a[1], a[3], a[5])), times(w2, plus(xy, xz, yz)))
    s1 = [
        plus(times(w1, d[1]), times(w2, plus(d[7], d[9], d[11], d[13]))),
        plus(times(w1, d[3]), times(w2, plus(minus(d[7], d[9]), d[15], d[17]))),
        plus(times(w1, d[5]), times(w2, plus(minus(d[11], d[13]), minus(d[15], d[17])))),
    ]
    sxx = plus(times(w1, a[1]), times(w2, plus(xy, xz)))
    syy = plus(times(w1, a[3]), times(w2, plus(xy, yz)))
    szz = plus(times(w1, a[5]), times(w2, plus(xz, yz)))
    sxy = times(w2, minus(a[7], a[9]))
    sxz = times(w2, minus(a[11], a[13]))
    syz = times(w2, minus(a[15], a[17]))
    rows = ((sxx, sxy, sxz), (sxy, syy, syz), (sxz, syz, szz))
    s2u = [plus(*(times(e, v) for e, v in zip(row, u))) for row in rows]
    dot = lambda p, q: plus(*(times(e, v) for e, v in zip(p, q)))
    uu = u[0] * u[0] + u[1] * u[1] + u[2] * u[2]
    m0 = plus(times(1.0 - 1.5 * uu, s0), times(3.0, dot(s1, u)), times(4.5, dot(s2u, u)))
    m = [
        minus(plus(times(3.0, s1[k]), times(9.0, s2u[k])), times(3.0, times(u[k], s0)))
        for k in range(3)
    ]
    t0 = plus(
        times(HEAT[0], g(19)), times(HEAT[1], plus(*(g(20 + k) for k in range(6))))
    )
    t1 = [times(HEAT[1], minus(g(20 + 2 * k), g(21 + 2 * k))) for k in range(3)]
    s = plus(t0, times(4.0, dot(t1, u)))
    p = [plus(times(OMEGA_F, m[k]), times(coef, t1[k])) for k in range(3)]
    base = times(fluid, minus(times(OMEGA_F, m0), dot(p, u)))
    p = [times(fluid, e) for e in p]
    relax_f, relax_t = (1.0 - OMEGA_F) * fluid, (1.0 - OMEGA_T) * fluid
    heat = times(fluid, times(OMEGA_T, s))
    out = {}
    for i in wanted:
        if i < 19:
            value = plus(times(relax_f, g(i)), base)
            for k in range(3):
                if C[i][k] == 1:
                    value = plus(value, p[k])
                elif C[i][k] == -1:
                    value = minus(value, p[k])
            out[i] = value
        else:
            out[i] = plus(times(relax_t, g(i)), heat)
    return out


def wall_of(m, rows, lanes, y_first, y_last):
    mask = None
    if C[m][1] != 0:
        mask = rows == (y_last if C[m][1] == 1 else y_first)
    if C[m][2] != 0:
        edge = lanes == (lanes.shape[1] - 1 if C[m][2] == 1 else 0)
        mask = edge if mask is None else mask | edge
    return mask


def shifted(slab, m, fill, rows):
    count, width = slab.shape
    if C[m][1] == 1:
        slab = jnp.where(rows == count - 1, fill, pltpu.roll(slab, count - 1, 0))
    elif C[m][1] == -1:
        slab = jnp.where(rows == 0, fill, pltpu.roll(slab, 1, 0))
    if C[m][2] != 0:
        slab = pltpu.roll(slab, width - 1 if C[m][2] == 1 else 1, 1)
    return slab


def bounce(m, own, pulled, link, wall):
    pulled = jnp.zeros_like(own) if pulled is None else pulled
    if m < 19:
        return jnp.where(link if wall is None else link | wall, own, pulled)
    if wall is not None:
        pulled = jnp.where(wall, own, pulled)
    return jnp.where(link, 1.0 - own, pulled)


def link_mask(packed, x, m):
    group, low = place(m if m < 19 else m - 19)
    return (packed[group, x] & (((1 << BITS) - 1) << low)) != 0


def indices(shape):
    return (
        lax.broadcasted_iota(jnp.int32, shape, 0),
        lax.broadcasted_iota(jnp.int32, shape, 1),
    )


def pick(even, first, second):
    return jnp.where(even, first, second)


SPAN_EVEN, STREAM_EVEN, Y_FIRST, Y_LAST, CONTROL = range(5)


def position(count_y):
    span, stream = lax.axis_index("span"), lax.axis_index("stream")
    at_end = span == lax.axis_size("span") - 1
    return (
        lax.rem(span, 2) == 0,
        lax.rem(stream, 2) == 0,
        jnp.where(span == 0, 0, -1),
        jnp.where(at_end, count_y - 1, -1),
        span * control_share(count_y),
    )


def control_share(count_y):
    return PERIOD_PARTS * (count_y // (SEGMENT_WIDTH + 2)) * SEGMENT_CONTROLS


def pack_span_kernel(field, out_a, out_b, lo, hi, sems):
    info = position(field.shape[2])
    rows = field.shape[2]
    copies = []
    for k in range(FACE):
        copies.append(pltpu.make_async_copy(field.at[YP[k], :, 0], lo.at[k], sems.at[k]))
        copies.append(
            pltpu.make_async_copy(field.at[YM[k], :, rows - 1], hi.at[k], sems.at[FACE + k])
        )
    for copy in copies:
        copy.start()
    for copy in copies:
        copy.wait()
    even = info[SPAN_EVEN]
    for k in range(FACE):
        out_a[k] = pick(even, hi[k], lo[k])
        out_b[k] = pick(even, lo[k], hi[k])
    out_a[FACE] = jnp.zeros_like(out_a[FACE])
    out_b[FACE] = jnp.zeros_like(out_b[FACE])


def prepare_kernel(primal, solid, links, state, packed, span_of, slots):
    count_x, count_y, depth = solid.shape
    info = position(count_y)
    cells = count_x * count_y * depth
    for x in range(count_x):
        f = [primal[m, x] for m in range(MEMBERS)]
        rho = plus(*f[:19])
        inverse = 1.0 / rho
        momentum = [
            minus(plus(*(f[i] for i in range(1, 19) if C[i][k] == 1)),
                  plus(*(f[i] for i in range(1, 19) if C[i][k] == -1)))
            for k in range(3)
        ]
        theta = plus(*f[19:])
        for k in range(3):
            state[k, x] = momentum[k] * inverse
        state[3, x] = (4.0 * OMEGA_T) * theta * inverse
        state[4, x] = (1 - solid[x]).astype(jnp.float32)
        state[5, x] = rho
        state[6, x] = theta
    given = links.shape[2]
    slots[...] = jnp.full(slots.shape, cells, jnp.int32)
    for k in range(3):
        slots[k : k + 1, 0:given] = links[k]
    cell, direction = slots[0:1, :], slots[1:2, :]
    control = slots[2:3, :] - info[CONTROL]
    used = cell < cells
    span_of[0] = jnp.min(jnp.where(used, control, 1 << 20))
    span_of[1] = jnp.max(jnp.where(used, control, -1))
    total = slots.shape[1]
    column = lax.shift_right_logical(cell, depth.bit_length() - 1)
    height = cell & (depth - 1)
    columns = count_x * count_y
    on_column = lax.broadcasted_iota(jnp.int32, (columns, total), 0) == column
    on_height = jnp.where(
        (lax.broadcasted_iota(jnp.int32, (depth, total), 0) == height) & used, 1.0, 0.0
    ).astype(jnp.bfloat16)
    for group in range(GROUPS):
        code = jnp.zeros((1, total), jnp.float32)
        for i in range(1, 19):
            if place(i)[0] == group:
                value = (control + 1).astype(jnp.float32) * float(1 << place(i)[1])
                code = jnp.where(direction == i, value, code)
        left = jnp.where(on_column, code, 0.0).astype(jnp.bfloat16)
        dense = lax.dot_general(
            left, on_height, (((1,), (1,)), ((), ())), preferred_element_type=jnp.float32
        )
        packed[group] = dense.astype(jnp.int32).reshape(count_x, count_y, depth)


def message_rows(count_y):
    return (2 * FACE + 5) * count_y + 8


def gather_pull(field, halo_lo, halo_hi, x, m, rows, beyond_lo=None, beyond_hi=None):
    count_x = halo_lo.shape[1] if hasattr(halo_lo, "shape") else 0
    at = x + C[m][0]
    if at < 0 or at >= count_x:
        beyond = beyond_lo if at < 0 else beyond_hi
        if beyond is None:
            return None
        slab, fill = beyond(m)
    else:
        slab = field(m, at)
        fill = None
        if C[m][1] == 1:
            fill = halo_hi[YP.index(m), at : at + 1]
        elif C[m][1] == -1:
            fill = halo_lo[YM.index(m), at : at + 1]
    return shifted(slab, m, fill, rows)


def advance_slab(field, halo_lo, halo_hi, state, packed, x, info, beyond_lo=None, beyond_hi=None):
    rows, lanes = indices(state.shape[2:])
    b = {0: field(0, x), 19: field(19, x)}
    for m in range(MEMBERS):
        if m in (0, 19):
            continue
        pulled = gather_pull(field, halo_lo, halo_hi, x, m, rows, beyond_lo, beyond_hi)
        wall = wall_of(m, rows, lanes, info[Y_FIRST], info[Y_LAST])
        b[m] = bounce(m, field(opp(m), x), pulled, link_mask(packed, x, m), wall)
    u = [state[k, x] for k in range(3)]
    return collide(b, u, state[3, x], state[4, x], range(MEMBERS))


def select_halos(even, recv_a, recv_b, lo, hi):
    hi[...] = pick(even, recv_a[...], recv_b[...])
    lo[...] = pick(even, recv_b[...], recv_a[...])


def edge_kernel(adjoint, recv_a, recv_b, state, packed, edge, out_a, out_b, lo, hi):
    count_x, count_y = state.shape[1:3]
    info = position(count_y)
    select_halos(info[SPAN_EVEN], recv_a, recv_b, lo, hi)
    field = lambda m, x: adjoint[m, x]
    even = info[STREAM_EVEN]
    for side, x, sent, flagged in ((0, 0, XP, XM), (1, count_x - 1, XM, XP)):
        out = advance_slab(field, lo, hi, state, packed, x, info)
        for m in range(MEMBERS):
            edge[side, m] = out[m]
        flags = state[4, x].astype(jnp.int32)
        for k, m in enumerate(flagged[: FACE - 1]):
            flags = flags + jnp.where(link_mask(packed, x, m), 2 << k, 0)
        parts = [adjoint[m, x] for m in sent] + [out[m] for m in sent]
        parts += [state[k, x] for k in range(4)] + [flags.astype(jnp.float32)]
        down = [m for m in sent if C[m][1] == -1][0]
        up = [m for m in sent if C[m][1] == 1][0]
        below, above = lo[YM.index(down), x : x + 1], hi[YP.index(up), x : x + 1]
        tail = jnp.concatenate(
            [below, above, jnp.zeros((6, below.shape[1]), jnp.float32)], axis=0
        )
        first = even if side == 1 else jnp.logical_not(even)

        def write(target):
            for k, part in enumerate(parts):
                target[k * count_y : (k + 1) * count_y] = part
            target[len(parts) * count_y : len(parts) * count_y + 8] = tail

        @pl.when(first)
        def _():
            write(out_a)

        @pl.when(jnp.logical_not(first))
        def _():
            write(out_b)


def interior_kernel(adjoint, recv_a, recv_b, state, packed, inner, lo, hi):
    count_x = state.shape[1]
    info = position(state.shape[2])
    select_halos(info[SPAN_EVEN], recv_a, recv_b, lo, hi)
    field = lambda m, x: adjoint[m, x]
    for x in range(1, count_x - 1):
        out = advance_slab(field, lo, hi, state, packed, x, info)
        for m in range(MEMBERS):
            inner[m, x - 1] = out[m]


def correct_kernel(
    adjoint, span_a, span_b, recv_a, recv_b, state, packed, edge, inner,
    fixed, ring, out_a, out_b, lo, hi, message, send,
):
    count_x, count_y = state.shape[1:3]
    info = position(count_y)
    select_halos(info[SPAN_EVEN], span_a, span_b, lo, hi)
    even = info[STREAM_EVEN]
    message[1] = pick(even, recv_a[...], recv_b[...])
    message[0] = pick(even, recv_b[...], recv_a[...])
    rows, lanes = indices(state.shape[2:])
    for side, x, came, went in ((0, 0, XM, XP), (1, count_x - 1, XP, XM)):
        part = lambda k: message[side, k * count_y : (k + 1) * count_y]
        tail = (2 * FACE + 5) * count_y
        b = {}
        for k, m in enumerate(came):
            row = tail if C[m][1] == -1 else tail + 1
            fill = message[side, row : row + 1] if C[m][1] != 0 else None
            pulled = shifted(part(k), m, fill, rows)
            blocked = link_mask(packed, x, m)
            wall = wall_of(m, rows, lanes, info[Y_FIRST], info[Y_LAST])
            blocked = blocked if wall is None else blocked | wall
            b[m] = jnp.where(blocked, 0.0, pulled)
        u = [state[k, x] for k in range(3)]
        out = collide(b, u, state[3, x], state[4, x], range(MEMBERS))
        for m in range(MEMBERS):
            fixed[side, m] = edge[side, m] + out[m]
        u = [part(2 * FACE + k) for k in range(3)]
        flags = part(2 * FACE + 4).astype(jnp.int32)
        b = {}
        for k, m in enumerate(went):
            fill = None
            if C[m][1] == 1:
                fill = hi[YP.index(m), x : x + 1]
            elif C[m][1] == -1:
                fill = lo[YM.index(m), x : x + 1]
            pulled = shifted(adjoint[m, x], m, fill, rows)
            blocked = (flags & (2 << (k % (FACE - 1)))) != 0
            wall = wall_of(m, rows, lanes, info[Y_FIRST], info[Y_LAST])
            blocked = blocked if wall is None else blocked | wall
            b[m] = jnp.where(blocked, 0.0, pulled)
        fluid = (flags & 1).astype(jnp.float32)
        out = collide(b, u, part(2 * FACE + 3), fluid, came)
        for k, m in enumerate(came):
            ring[side, k] = part(FACE + k) + out[m]
    last = count_y - 1
    for side, group, row in ((0, YP, 0), (1, YM, last)):
        for k, m in enumerate(group):
            send[side, k, 0:1] = fixed[0, m, row : row + 1]
            send[side, k, count_x - 1 : count_x] = fixed[1, m, row : row + 1]
            for x in range(1, count_x - 1):
                send[side, k, x : x + 1] = inner[m, x - 1, row : row + 1]
        send[side, FACE] = jnp.zeros((count_x, state.shape[3]), jnp.float32)
        for end, came in ((0, XM), (1, XP)):
            m = [e for e in came if e in group][0]
            send[side, FACE, end : end + 1] = ring[end, came.index(m), row : row + 1]
    span_even = info[SPAN_EVEN]
    out_a[...] = pick(span_even, send[1], send[0])
    out_b[...] = pick(span_even, send[0], send[1])


CHUNK = 4


def sensitivity_kernel(span_of, primal, state, packed, fixed, inner, out, values, owners, acc):
    count_x, count_y, depth = state.shape[1:]
    info = position(count_y)

    def field(m, x):
        if x == 0 or x == count_x - 1:
            return fixed[0 if x == 0 else 1, m]
        return inner[m, x - 1]

    for x in range(count_x):
        u = [state[k, x] for k in range(3)]
        rho, theta = state[5, x], state[6, x]
        base = 1.0 - 1.5 * (u[0] * u[0] + u[1] * u[1] + u[2] * u[2])
        for i in range(1, 19):
            cu = None
            for k in range(3):
                cu = plus(cu, u[k]) if C[i][k] == 1 else minus(cu, u[k]) if C[i][k] == -1 else cu
            target = (OMEGA_F * WEIGHTS[i]) * rho * (base + cu * (3.0 + 4.5 * cu))
            value = ((1.0 - OMEGA_F) * primal[i, x] + target) * field(opp(i), x)
            if i <= 6:
                target = (OMEGA_T * HEAT[i]) * theta * (1.0 + 4.0 * cu)
                heat = (1.0 - OMEGA_T) * primal[19 + i, x] + target
                value = value + heat * (1.0 - field(19 + opp(i), x))
            group, low = place(i)
            owner = lax.shift_right_logical(packed[group, x], low) & ((1 << BITS) - 1)
            at = ((i - 1) * count_x + x) * count_y
            values[at : at + count_y] = value
            owners[at : at + count_y] = owner - 1
    acc[...] = jnp.zeros_like(acc)
    first, last = span_of[0], span_of[1]
    passes = lax.div(jnp.maximum(last - first + CHUNK, 0), CHUNK)
    step = 64

    def one_pass(j, carry):
        q = first + j * CHUNK

        def block(n, sums):
            sums = list(sums)
            start = pl.multiple_of(n * step, step)
            for t in range(step // 8):
                v = values[pl.ds(start + 8 * t, 8)]
                o = owners[pl.ds(start + 8 * t, 8)]
                for c in range(CHUNK):
                    sums[c] = sums[c] + jnp.where(o == q + c, v, 0.0)
            return tuple(sums)

        zero = jnp.zeros((8, depth), jnp.float32)
        sums = lax.fori_loop(0, values.shape[0] // step, block, (zero,) * CHUNK)
        for c in range(CHUNK):
            row = jnp.minimum(info[CONTROL] + q + c, acc.shape[0] - 1)
            inside = (q + c <= last).astype(jnp.float32)
            acc[pl.ds(row, 1)] = acc[pl.ds(row, 1)] + inside * jnp.sum(
                sums[c], axis=0, keepdims=True
            )
        return carry

    lax.fori_loop(0, passes, one_pass, 0)
    total = lax.dot_general(
        jnp.ones((8, depth), jnp.float32),
        acc[...],
        (((1,), (1,)), ((), ())),
        precision=lax.Precision.HIGHEST,
        preferred_element_type=jnp.float32,
    )
    out[...] = jnp.broadcast_to(total[:1], out.shape[::2])[:, None, :]


def total_kernel(copies, out):
    periods = lax.axis_size("stream") // PERIOD_PARTS
    total = jnp.sum(copies[...], axis=0) * (SENS_SCALE / periods)
    out[...] = total[:, : out.shape[1]]


def final_kernel(fixed, inner, ring, span_a, span_b, state, packed, out, lo, hi):
    count_x = state.shape[1]
    info = position(state.shape[2])
    select_halos(info[SPAN_EVEN], span_a, span_b, lo, hi)

    def field(m, x):
        if x == 0 or x == count_x - 1:
            return fixed[0 if x == 0 else 1, m]
        return inner[m, x - 1]

    def beyond(end, came, m):
        fill = None
        if C[m][1] != 0:
            fill = (hi if C[m][1] == 1 else lo)[FACE, end : end + 1]
        return ring[end, came.index(m)], fill

    for x in range(count_x):
        result = advance_slab(
            field, lo, hi, state, packed, x, info,
            functools.partial(beyond, 0, XM), functools.partial(beyond, 1, XP),
        )
        for m in range(MEMBERS):
            out[m, x] = result[m]


def vmem():
    return pl.BlockSpec(memory_space=pltpu.VMEM)


def smem():
    return pl.BlockSpec(memory_space=pltpu.SMEM)


def f32(*shape):
    return jax.ShapeDtypeStruct(shape, jnp.float32)


def run(kernel, inputs, in_specs, outs, scratch=(), out_specs=None, limit=12 << 20):
    nbytes = sum(4 * e.size for e in inputs) + sum(4 * e.size for e in outs)
    return pl.pallas_call(
        kernel,
        out_shape=tuple(outs),
        in_specs=in_specs,
        out_specs=tuple(out_specs or [vmem()] * len(outs)),
        scratch_shapes=list(scratch),
        cost_estimate=pl.CostEstimate(
            flops=2 * nbytes, bytes_accessed=nbytes, transcendentals=0
        ),
        compiler_params=pltpu.CompilerParams(vmem_limit_bytes=limit),
    )(*inputs)


def swap_pairs(count, start, closed):
    pairs = []
    for i in range(start, count if closed else count - 1, 2):
        j = (i + 1) % count
        pairs += [(i, j), (j, i)]
    return pairs


def swap(parts, axis, closed):
    count = lax.axis_size(axis)
    assert count % 2 == 0
    return [
        lax.ppermute(part, axis, swap_pairs(count, start, closed))
        for start, part in enumerate(parts)
    ]


def shards(primal, adjoint, solid, links):
    members, count_x, count_y, depth = adjoint.shape
    assert members == MEMBERS and depth == 128 and count_y % 8 == 0
    stream_count, span_count = lax.axis_size("stream"), lax.axis_size("span")
    controls = control_share(count_y) * span_count
    assert control_share(count_y) < (1 << BITS) - 1 and controls <= depth
    row = (count_x, depth)
    halo = f32(FACE + 1, *row)
    halo_scratch = [pltpu.VMEM(halo.shape, jnp.float32)] * 2
    slab = (count_y, depth)

    span_a, span_b = swap(
        run(
            pack_span_kernel,
            [adjoint],
            [pl.BlockSpec(memory_space=pl.ANY)],
            [halo, halo],
            [pltpu.VMEM((FACE, *row), jnp.float32)] * 2 + [pltpu.SemaphoreType.DMA((2 * FACE,))],
        ),
        "span",
        False,
    )
    slots = -(-links.shape[2] // 128) * 128
    state, packed, span_of = run(
        prepare_kernel,
        [primal, solid, links],
        [vmem()] * 3,
        [
            f32(7, count_x, *slab),
            jax.ShapeDtypeStruct((GROUPS, count_x, *slab), jnp.int32),
            jax.ShapeDtypeStruct((2,), jnp.int32),
        ],
        [pltpu.VMEM((8, slots), jnp.int32)],
        [vmem(), vmem(), smem()],
    )
    message = f32(message_rows(count_y), depth)
    edge, *parts = run(
        edge_kernel,
        [adjoint, span_a, span_b, state, packed],
        [vmem()] * 5,
        [f32(2, MEMBERS, *slab), message, message],
        halo_scratch,
    )
    stream_a, stream_b = swap(parts, "stream", True)
    (inner,) = run(
        interior_kernel,
        [adjoint, span_a, span_b, state, packed],
        [vmem()] * 5,
        [f32(MEMBERS, count_x - 2, *slab)],
        halo_scratch,
    )
    fixed, ring, *parts = run(
        correct_kernel,
        [adjoint, span_a, span_b, stream_a, stream_b, state, packed, edge, inner],
        [vmem()] * 9,
        [f32(2, MEMBERS, *slab), f32(2, FACE, *slab), halo, halo],
        halo_scratch
        + [
            pltpu.VMEM((2, *message.shape), jnp.float32),
            pltpu.VMEM((2, *halo.shape), jnp.float32),
        ],
    )
    next_a, next_b = swap(parts, "span", False)
    (partial,) = run(
        sensitivity_kernel,
        [span_of, primal, state, packed, fixed, inner],
        [smem()] + [vmem()] * 5,
        [f32(stream_count * span_count, 1, depth)],
        [
            pltpu.VMEM((18 * count_x * count_y, depth), jnp.float32),
            pltpu.VMEM((18 * count_x * count_y, depth), jnp.int32),
            pltpu.VMEM((depth, depth), jnp.float32),
        ],
    )
    copies = lax.all_to_all(partial, ("stream", "span"), 0, 0, tiled=True)
    (sensitivity,) = run(total_kernel, [copies], [vmem()], [f32(1, controls)])
    (result,) = run(
        final_kernel,
        [fixed, inner, ring, next_a, next_b, state, packed],
        [vmem()] * 7,
        [f32(MEMBERS, count_x, *slab)],
        halo_scratch,
    )
    return result, sensitivity.reshape(controls)


def solution(mesh):
    placed = (
        P(None, "stream", "span", None),
        P(None, "stream", "span", None),
        P("stream", "span", None),
        P(None, "stream", "span"),
    )
    return jax.shard_map(
        shards,
        mesh=mesh,
        in_specs=placed,
        out_specs=(P(None, "stream", "span", None), P()),
        check_vma=False,
    )
```
